128 devices in a mesh: expert: 16 (over x, y_hi, core), dp: 8 (over z, y_lo).
Axes of the slice: x: 4, y: 4 (y_hi: 2, y_lo: 2; y = y_hi * 2 + y_lo), z: 4, core: 2. Of those that a mesh axis runs over, the one named last changes fastest.
Arguments:
- tokens: bfloat16 [16384, 4096], P(('expert', 'dp')), may hold values from -6 to 6
- cotangent: bfloat16 [16384, 4096], P(('expert', 'dp')), may hold values from -6 to 6
- expert_ids: int32 [16384, 2], P(('expert', 'dp')), may hold values from 0 to 15, all different within a row; in each aligned block of 128 rows (0 to 127, 128 to 255, ...) at most 32 rows name the same one
- router_w: bfloat16 [4096, 16], replicated, may hold values from -0.09375 to 0.09375
- w_gate: bfloat16 [16, 4096, 768], P('expert'), may hold values from -0.09375 to 0.09375
- w_up: bfloat16 [16, 4096, 768], P('expert'), may hold values from -0.09375 to 0.09375
- w_down: bfloat16 [16, 4096, 768], P('expert'), may hold values from -0.21875 to 0.21875
Outputs:
- output: bfloat16 [16384, 4096], P(('expert', 'dp'))
- d_tokens: bfloat16 [16384, 4096], P(('expert', 'dp'))
- router_grad: float32 [4096, 16], replicated
- gate_grad: bfloat16 [16, 4096, 768], P('expert', 'dp')
- up_grad: bfloat16 [16, 4096, 768], P('expert', 'dp')
- down_grad: bfloat16 [16, 4096, 768], P('expert', 'dp')
The draws below stay inside these ranges and needn't reach their ends.
Inputs may be any that keep to these rules, and one draw needn't show every extreme that they name: `expert_ids`: each row names 2 different experts. Within each aligned block of 128 rows (the tokens of one device) no expert is named more than 32 times, a bound that some block reaches.
All inputs are finite; a program needn't handle non-finite values.
Results may differ from the reference program's by a relative error of at most 0.014.
Values may be sent and summed in bfloat16 or wider, within the bound.
A program may use at most 192 MiB of HBM per device.

```python
import math
import jax
import jax.numpy as jnp
import numpy as np
from jax import lax

D = 4096
HID = 768
TOP = 2
T_DEV = 128
EXPERTS = 16
CAP = 32
TOKENS = 16384
N_EXPERT = 16
N_DP = 8


def levels(key, dims, cuts, least, top_value):
    gain = 1.0
    for axis_at, blocks in cuts:
        steps = jax.random.uniform(jax.random.fold_in(jax.random.fold_in(key, 6), axis_at), (blocks,), jnp.float32, least / len(cuts), top_value / len(cuts))
        gain = gain * jnp.repeat(jnp.exp(steps), dims[axis_at] // blocks).reshape((-1,) + (1,) * (len(dims) - 1 - axis_at))
    return gain


def assign_block(key, own, number, rows, number_of, top, bound, lean):
    sequence = jax.random.permutation(key, number_of)
    crowded, common = portions_of(number_of, rows * top, bound, lean, True), portions_of(number_of, rows * top, bound, lean, False)
    places = jnp.arange(number_of)

    def named(tallies, turn):
        used = int((tallies > 0).sum())
        fixed = max(1, used // 4)
        moved = fixed + (places - fixed + turn * (used - fixed)) % max(1, number_of - fixed)
        return jnp.zeros((number_of,), jnp.int32).at[sequence[jnp.where(places < fixed, places, moved)]].set(jnp.asarray(tallies, jnp.int32))

    tallies = jnp.where(number % 4 == 0, named(crowded, number // 4), named(common, number - number // 4 - 1))
    mixed = jax.random.permutation(jax.random.fold_in(own, 3), number_of)
    source_of, sink = mixed[0:number_of // 2 * 2:2], mixed[1:number_of // 2 * 2:2]
    margin = jnp.minimum(tallies[source_of] - 1, bound - tallies[sink]) // 2
    margin = jnp.where((source_of == sequence[0]) | (sink == sequence[0]) | (tallies[sink] == 0), 0, jnp.maximum(margin, 0))
    moved = jax.random.randint(jax.random.fold_in(own, 4), (number_of // 2,), 0, 1 << 20) % (margin + 1)
    tallies = tallies.at[source_of].add(-moved).at[sink].add(moved)
    labels = jnp.searchsorted(jnp.cumsum(tallies), jnp.arange(rows * top), side="right").astype(jnp.int32)
    grid = labels.reshape(top, rows).T
    grid = grid[jax.random.permutation(jax.random.fold_in(own, 1), rows)]
    turn = jax.random.randint(jax.random.fold_in(own, 2), (rows, 1), 0, top)
    return jnp.take_along_axis(grid, (jnp.arange(top)[None, :] + turn) % top, axis=1)


def portions_of(amount, total, limit, lean, full):
    loads = [(1 << 20) // math.isqrt(rank ** lean) + 1 for rank in range(1, amount + 1)]
    largest = limit if full else min(limit, max(-(-total // amount), total * loads[0] // sum(loads)))
    least = 1 if total - largest >= amount - 1 else 0
    holding, surplus = [largest] + [least] * (amount - 1), total - largest - least * (amount - 1)
    while surplus > 0:
        movable = [i for i in range(1, amount) if holding[i] < largest] or [i for i in range(1, amount) if holding[i] < limit]
        mass, remaining = sum([loads[i] for i in movable]), surplus
        for i in movable:
            extra = min(limit - holding[i], max(1, remaining * loads[i] // mass), surplus)
            holding[i] = holding[i] + extra
            surplus = surplus - extra
    return np.array(holding)


def noise(key, dims, deviation, bound, shards=(), held_as=jnp.bfloat16):
    values = deviation * jax.random.normal(key, dims, jnp.float32)
    if shards:
        values = values * levels(key, dims, shards, -0.22, 0.18)
    return jnp.clip(values, -bound, bound).astype(held_as)


def setup_inputs(seed: int = 0) -> dict:
    seeds = jax.random.split(jax.random.key(seed), 8)
    tokens = noise(seeds[0], (TOKENS, D), 1.0, 6.0, ((0, 128),))
    cotangent = noise(seeds[1], (TOKENS, D), 1.0, 6.0, ((0, 128),))
    expert_ids_keys = jax.random.split(jax.random.fold_in(seeds[2], 1), TOKENS // T_DEV)
    expert_ids_turns = jax.random.permutation(jax.random.fold_in(seeds[2], 3), TOKENS // T_DEV)
    expert_ids = jax.vmap(lambda own, number: assign_block(jax.random.fold_in(seeds[2], 2), own, number, T_DEV, EXPERTS, TOP, CAP, 2))(expert_ids_keys, expert_ids_turns).reshape((TOKENS, TOP))
    router_w = noise(seeds[3], (D, EXPERTS), D ** -0.5, 0.09375)
    w_gate = noise(seeds[4], (EXPERTS, D, HID), D ** -0.5, 0.09375, ((0, 16),))
    w_up = noise(seeds[5], (EXPERTS, D, HID), D ** -0.5, 0.09375, ((0, 16),))
    w_down = noise(seeds[6], (EXPERTS, D, HID), HID ** -0.5, 0.21875, ((0, 16),))
    return {"tokens": tokens, "cotangent": cotangent, "expert_ids": expert_ids, "router_w": router_w, "w_gate": w_gate, "w_up": w_up, "w_down": w_down}


def slot_positions(expert_ids, expert_count, capacity):
    row_count, top_count = expert_ids.shape
    flat_ids = expert_ids.reshape(row_count * top_count).astype(jnp.int32)
    onehot = (flat_ids[:, None] == jnp.arange(expert_count, dtype=jnp.int32)[None, :]).astype(jnp.int32)
    before = jnp.cumsum(onehot, axis=0) - onehot
    rank_in = jnp.sum(before * onehot, axis=1).astype(jnp.int32)
    return (flat_ids * capacity + rank_in).astype(jnp.int32)


def owner_table(flat_slots, slot_count):
    entry_count = flat_slots.shape[0]
    owners = jnp.full((slot_count,), entry_count, dtype=jnp.int32)
    return owners.at[flat_slots].set(jnp.arange(entry_count, dtype=jnp.int32))


def padded_rows(values, row_index):
    zero_row = jnp.zeros((1, values.shape[1]), values.dtype)
    return jnp.concatenate([values, zero_row], axis=0)[row_index]


def expert_forward(source_rows, gate_w, up_w, down_w):
    gate_pre = jnp.einsum("jcd,dh->jch", source_rows.astype(jnp.float32), gate_w.astype(jnp.float32))
    up_pre = jnp.einsum("jcd,dh->jch", source_rows.astype(jnp.float32), up_w.astype(jnp.float32))
    hidden = (jax.nn.silu(gate_pre) * up_pre).astype(jnp.bfloat16)
    expert_out = jnp.einsum("jch,dh->jcd", hidden.astype(jnp.float32), down_w.astype(jnp.float32)).astype(jnp.bfloat16)
    return expert_out, hidden, gate_pre, up_pre


def expert_backward(grad_rows, hidden, gate_pre, up_pre, gate_w, up_w, down_w):
    grad_hidden = jnp.einsum("jcd,dh->jch", grad_rows.astype(jnp.float32), down_w.astype(jnp.float32))
    sigmoid_gate = jax.nn.sigmoid(gate_pre)
    grad_gate = (grad_hidden * up_pre * sigmoid_gate * (1.0 + gate_pre * (1.0 - sigmoid_gate))).astype(jnp.bfloat16)
    grad_up = (grad_hidden * jax.nn.silu(gate_pre)).astype(jnp.bfloat16)
    grad_in = jnp.einsum("jch,dh->jcd", grad_gate.astype(jnp.float32), gate_w.astype(jnp.float32))
    grad_in = grad_in + jnp.einsum("jch,dh->jcd", grad_up.astype(jnp.float32), up_w.astype(jnp.float32))
    return grad_in.astype(jnp.bfloat16), grad_gate, grad_up


def reference(tokens, cotangent, expert_ids, router_w, w_gate, w_up, w_down):
    expert_count = N_EXPERT
    replica_count = N_DP
    row_count = T_DEV
    top_count = TOP
    feature_count = D
    capacity = CAP
    slot_count = expert_count * capacity
    logits = jnp.dot(tokens, router_w, preferred_element_type=jnp.float32)
    chosen = jnp.take_along_axis(logits, expert_ids, axis=1)
    route_probs = jax.nn.sigmoid(2.0 * chosen - jnp.sum(chosen, axis=1, keepdims=True))
    columns = jnp.arange(EXPERTS, dtype=jnp.int32)

    def split_rep(array):
        return jnp.swapaxes(array.reshape((expert_count, replica_count, row_count) + array.shape[1:]), 0, 1)

    def one_replica(totals, packed):
        gate_acc, up_acc, down_acc, router_acc = totals
        tok_rep, cot_rep, ids_rep, prob_rep = packed
        flat_slots = jax.vmap(lambda ids_block: slot_positions(ids_block, expert_count, capacity))(ids_rep)
        owners = jax.vmap(lambda slot_block: owner_table(slot_block, slot_count))(flat_slots)
        outbound = jax.vmap(lambda source_tok, owner_block: padded_rows(source_tok, owner_block // top_count))(tok_rep, owners)
        inbound = jnp.swapaxes(outbound.reshape(expert_count, expert_count, capacity, feature_count), 0, 1)

        def forward_block(pieces):
            return expert_forward(*pieces)

        expert_out, hidden, gate_pre, up_pre = lax.map(forward_block, (inbound, w_gate, w_up, w_down))
        returned = jnp.swapaxes(expert_out, 0, 1).reshape(expert_count, slot_count, feature_count)
        routed = jax.vmap(lambda back_block, slot_block: back_block[slot_block])(returned, flat_slots)
        routed = routed.reshape(expert_count, row_count, top_count, feature_count)
        output = jnp.sum(prob_rep[..., None] * routed.astype(jnp.float32), axis=2).astype(jnp.bfloat16)
        grad_prob = jnp.einsum("jtd,jtkd->jtk", cot_rep.astype(jnp.float32), routed.astype(jnp.float32))
        mixed = jnp.sum(prob_rep * grad_prob, axis=2, keepdims=True)
        grad_chosen = prob_rep * (grad_prob - mixed)
        match = (ids_rep[..., None] == columns).astype(jnp.float32)
        grad_logits = jnp.sum(grad_chosen[..., None] * match, axis=2).astype(jnp.bfloat16)
        router_acc = router_acc + jnp.einsum("jtd,jte->de", tok_rep.astype(jnp.float32), grad_logits.astype(jnp.float32))
        weighted = (prob_rep[..., None] * cot_rep[:, :, None, :].astype(jnp.float32)).astype(jnp.bfloat16)
        weighted = weighted.reshape(expert_count, row_count * top_count, feature_count)
        grad_out = jax.vmap(padded_rows)(weighted, owners)
        grad_inbound = jnp.swapaxes(grad_out.reshape(expert_count, expert_count, capacity, feature_count), 0, 1)

        def backward_block(pieces):
            grad_rows, in_rows, hid_rows, gate_rows, up_rows, gate_w, up_w, down_w = pieces
            grad_in, grad_gate, grad_up = expert_backward(grad_rows, hid_rows, gate_rows, up_rows, gate_w, up_w, down_w)
            gate_part = jnp.einsum("jcd,jch->dh", in_rows.astype(jnp.float32), grad_gate.astype(jnp.float32)).astype(jnp.bfloat16)
            up_part = jnp.einsum("jcd,jch->dh", in_rows.astype(jnp.float32), grad_up.astype(jnp.float32)).astype(jnp.bfloat16)
            down_part = jnp.einsum("jcd,jch->dh", grad_rows.astype(jnp.float32), hid_rows.astype(jnp.float32)).astype(jnp.bfloat16)
            return grad_in, gate_part, up_part, down_part

        grad_in, gate_part, up_part, down_part = lax.map(
            backward_block, (grad_inbound, inbound, hidden, gate_pre, up_pre, w_gate, w_up, w_down))
        gate_part, up_part, down_part = lax.optimization_barrier((gate_part, up_part, down_part))
        gate_acc = gate_acc + gate_part.astype(jnp.float32)
        up_acc = up_acc + up_part.astype(jnp.float32)
        down_acc = down_acc + down_part.astype(jnp.float32)
        grad_back = jnp.swapaxes(grad_in, 0, 1).reshape(expert_count, slot_count, feature_count)
        grad_routed = jax.vmap(lambda back_block, slot_block: back_block[slot_block])(grad_back, flat_slots)
        grad_routed = grad_routed.reshape(expert_count, row_count, top_count, feature_count)
        grad_tokens = jnp.sum(grad_routed.astype(jnp.float32), axis=2)
        grad_tokens = grad_tokens + jnp.einsum("jte,de->jtd", grad_logits.astype(jnp.float32), router_w.astype(jnp.float32))
        return (gate_acc, up_acc, down_acc, router_acc), (output, grad_tokens.astype(jnp.bfloat16))

    start = (jnp.zeros((EXPERTS, D, HID), jnp.float32), jnp.zeros((EXPERTS, D, HID), jnp.float32),
             jnp.zeros((EXPERTS, D, HID), jnp.float32), jnp.zeros((D, EXPERTS), jnp.float32))
    totals, stacked = lax.scan(one_replica, start,
                               (split_rep(tokens), split_rep(cotangent), split_rep(expert_ids), split_rep(route_probs)))
    gate_acc, up_acc, down_acc, router_acc = totals
    output = jnp.swapaxes(stacked[0], 0, 1).reshape(TOKENS, D)
    d_tokens = jnp.swapaxes(stacked[1], 0, 1).reshape(TOKENS, D)
    router_grad = router_acc / replica_count
    gate_grad = (gate_acc / replica_count).astype(jnp.bfloat16)
    up_grad = (up_acc / replica_count).astype(jnp.bfloat16)
    down_grad = (down_acc / replica_count).astype(jnp.bfloat16)
    return (output, d_tokens, router_grad, gate_grad, up_grad, down_grad)
```

```python
import jax
import jax.numpy as jnp
from jax import lax
from jax.sharding import PartitionSpec as P


def slot_positions(expert_ids, expert_count, capacity):
    row_count, top_count = expert_ids.shape
    flat_ids = expert_ids.reshape(row_count * top_count)
    onehot = (flat_ids[:, None] == jnp.arange(expert_count, dtype=jnp.int32)[None, :]).astype(
        jnp.int32
    )
    before = jnp.cumsum(onehot, axis=0) - onehot
    rank_in = jnp.sum(before * onehot, axis=1)
    return flat_ids * capacity + rank_in


def owner_table(flat_slots, slot_count):
    entry_count = flat_slots.shape[0]
    owners = jnp.full((slot_count,), entry_count, dtype=jnp.int32)
    return owners.at[flat_slots].set(jnp.arange(entry_count, dtype=jnp.int32))


def padded_rows(values, row_index):
    zero_row = jnp.zeros((1, values.shape[1]), values.dtype)
    return jnp.concatenate([values, zero_row], axis=0)[row_index]


def expert_forward(source_rows, expert_weights):
    gate_w, up_w, down_w = expert_weights
    gate_pre = jnp.einsum("...d,dh->...h", source_rows, gate_w, preferred_element_type=jnp.float32)
    up_pre = jnp.einsum("...d,dh->...h", source_rows, up_w, preferred_element_type=jnp.float32)
    hidden = (jax.nn.silu(gate_pre) * up_pre).astype(jnp.bfloat16)
    expert_out = jnp.einsum(
        "...h,dh->...d", hidden, down_w, preferred_element_type=jnp.float32
    ).astype(jnp.bfloat16)
    return (expert_out, hidden, gate_pre, up_pre)


def expert_backward(grad_rows, gate_pre, up_pre, expert_weights):
    gate_w, up_w, down_w = expert_weights
    grad_hidden = jnp.einsum("...d,dh->...h", grad_rows, down_w, preferred_element_type=jnp.float32)
    sigmoid_gate = jax.nn.sigmoid(gate_pre)
    grad_gate = (
        grad_hidden * up_pre * sigmoid_gate * (1.0 + gate_pre * (1.0 - sigmoid_gate))
    ).astype(jnp.bfloat16)
    grad_up = (grad_hidden * jax.nn.silu(gate_pre)).astype(jnp.bfloat16)
    grad_in = jnp.einsum("...h,dh->...d", grad_gate, gate_w, preferred_element_type=jnp.float32)
    grad_in = grad_in + jnp.einsum(
        "...h,dh->...d", grad_up, up_w, preferred_element_type=jnp.float32
    )
    return (grad_in.astype(jnp.bfloat16), grad_gate, grad_up)


def on_device(tokens, cotangent, expert_ids, router_w, w_gate, w_up, w_down):
    row_count, top_count = expert_ids.shape
    feature_count = tokens.shape[1]
    expert_count = lax.axis_size("expert")
    replica_count = lax.axis_size("dp")
    capacity = 2 * row_count * top_count // expert_count
    slot_count = expert_count * capacity
    expert_weights = (w_gate[0], w_up[0], w_down[0])
    logits = jnp.dot(tokens, router_w, preferred_element_type=jnp.float32)
    chosen = jnp.take_along_axis(logits, expert_ids, axis=1)
    route_probs = jax.nn.sigmoid(2.0 * chosen - jnp.sum(chosen, axis=1, keepdims=True))
    flat_slots = slot_positions(expert_ids, expert_count, capacity)
    owners = owner_table(flat_slots, slot_count)
    outbound = padded_rows(tokens, owners // top_count).reshape(
        expert_count, capacity, feature_count
    )
    weighted = (route_probs[:, :, None] * cotangent[:, None, :].astype(jnp.float32)).astype(
        jnp.bfloat16
    )
    weighted = weighted.reshape(row_count * top_count, feature_count)
    grad_out = padded_rows(weighted, owners).reshape(expert_count, capacity, feature_count)
    sent = jnp.stack([outbound, grad_out], axis=1)
    arrived = lax.all_to_all(sent, "expert", split_axis=0, concat_axis=0, tiled=True)
    received = arrived[:, 0]
    grad_recv = arrived[:, 1]
    expert_out, hidden, gate_pre, up_pre = expert_forward(received, expert_weights)
    grad_in, grad_gate, grad_up = expert_backward(grad_recv, gate_pre, up_pre, expert_weights)
    back = lax.all_to_all(
        jnp.stack([expert_out, grad_in], axis=1), "expert", split_axis=0, concat_axis=0, tiled=True
    )
    returned = back[:, 0].reshape(slot_count, feature_count)
    grad_back = back[:, 1].reshape(slot_count, feature_count)
    routed = returned[flat_slots].reshape(row_count, top_count, feature_count)
    output = jnp.sum(route_probs[:, :, None] * routed.astype(jnp.float32), axis=1).astype(
        jnp.bfloat16
    )
    grad_prob = jnp.einsum("td,tkd->tk", cotangent, routed, preferred_element_type=jnp.float32)
    mixed = jnp.sum(route_probs * grad_prob, axis=1, keepdims=True)
    grad_chosen = route_probs * (grad_prob - mixed)
    columns = jnp.arange(router_w.shape[1], dtype=jnp.int32)
    match = (expert_ids[:, :, None] == columns[None, None, :]).astype(jnp.float32)
    grad_logits = jnp.sum(grad_chosen[:, :, None] * match, axis=1).astype(jnp.bfloat16)
    router_part = jnp.dot(tokens.T, grad_logits, preferred_element_type=jnp.float32)
    router_grad = lax.psum(router_part, ("expert", "dp")) / replica_count
    grad_tokens = jnp.sum(
        grad_back[flat_slots].reshape(row_count, top_count, feature_count).astype(jnp.float32),
        axis=1,
    )
    grad_tokens = grad_tokens + jnp.dot(grad_logits, router_w.T, preferred_element_type=jnp.float32)
    d_tokens = grad_tokens.astype(jnp.bfloat16)
    gate_part = jnp.einsum("nkd,nkh->dh", received, grad_gate, preferred_element_type=jnp.float32)
    up_part = jnp.einsum("nkd,nkh->dh", received, grad_up, preferred_element_type=jnp.float32)
    down_part = jnp.einsum("nkd,nkh->dh", grad_recv, hidden, preferred_element_type=jnp.float32)
    gate_total, up_total, down_total = (
        lax.psum_scatter(
            gate_part.astype(jnp.bfloat16), "dp", scatter_dimension=0, tiled=True
        ).astype(jnp.float32),
        lax.psum_scatter(
            up_part.astype(jnp.bfloat16), "dp", scatter_dimension=0, tiled=True
        ).astype(jnp.float32),
        lax.psum_scatter(
            down_part.astype(jnp.bfloat16), "dp", scatter_dimension=0, tiled=True
        ).astype(jnp.float32),
    )
    gate_grad = (gate_total / replica_count).astype(jnp.bfloat16)[None]
    up_grad = (up_total / replica_count).astype(jnp.bfloat16)[None]
    down_grad = (down_total / replica_count).astype(jnp.bfloat16)[None]
    return (output, d_tokens, router_grad, gate_grad, up_grad, down_grad)


def solution(mesh):
    placed = (
        P(("expert", "dp"), None),
        P(("expert", "dp"), None),
        P(("expert", "dp"), None),
        P(),
        P("expert", None, None),
        P("expert", None, None),
        P("expert", None, None),
    )
    return jax.shard_map(
        on_device,
        mesh=mesh,
        in_specs=placed,
        out_specs=(
            P(("expert", "dp"), None),
            P(("expert", "dp"), None),
            P(),
            P("expert", "dp", None),
            P("expert", "dp", None),
            P("expert", "dp", None),
        ),
        check_vma=False,
    )
```

```python
import jax
import jax.numpy as jnp
from jax import lax
from jax.sharding import PartitionSpec as P


def slot_positions(expert_ids, expert_count, capacity):
    row_count, top_count = expert_ids.shape
    flat_ids = expert_ids.reshape(row_count * top_count)
    onehot = (flat_ids[:, None] == jnp.arange(expert_count, dtype=jnp.int32)[None, :]).astype(
        jnp.int32
    )
    before = jnp.cumsum(onehot, axis=0) - onehot
    rank_in = jnp.sum(before * onehot, axis=1)
    return flat_ids * capacity + rank_in


def owner_table(flat_slots, slot_count):
    entry_count = flat_slots.shape[0]
    owners = jnp.full((slot_count,), entry_count, dtype=jnp.int32)
    return owners.at[flat_slots].set(jnp.arange(entry_count, dtype=jnp.int32))


def padded_rows(values, row_index):
    zero_row = jnp.zeros((1, values.shape[1]), values.dtype)
    return jnp.concatenate([values, zero_row], axis=0)[row_index]


def expert_forward(source_rows, expert_weights):
    gate_w, up_w, down_w = expert_weights
    gate_pre = jnp.einsum("...d,dh->...h", source_rows, gate_w, preferred_element_type=jnp.float32)
    up_pre = jnp.einsum("...d,dh->...h", source_rows, up_w, preferred_element_type=jnp.float32)
    hidden = (jax.nn.silu(gate_pre) * up_pre).astype(jnp.bfloat16)
    expert_out = jnp.einsum(
        "...h,dh->...d", hidden, down_w, preferred_element_type=jnp.float32
    ).astype(jnp.bfloat16)
    return (expert_out, hidden, gate_pre, up_pre)


def expert_backward(grad_rows, gate_pre, up_pre, expert_weights):
    gate_w, up_w, down_w = expert_weights
    grad_hidden = jnp.einsum("...d,dh->...h", grad_rows, down_w, preferred_element_type=jnp.float32)
    sigmoid_gate = jax.nn.sigmoid(gate_pre)
    grad_gate = (
        grad_hidden * up_pre * sigmoid_gate * (1.0 + gate_pre * (1.0 - sigmoid_gate))
    ).astype(jnp.bfloat16)
    grad_up = (grad_hidden * jax.nn.silu(gate_pre)).astype(jnp.bfloat16)
    grad_in = jnp.einsum("...h,dh->...d", grad_gate, gate_w, preferred_element_type=jnp.float32)
    grad_in = grad_in + jnp.einsum(
        "...h,dh->...d", grad_up, up_w, preferred_element_type=jnp.float32
    )
    return (grad_in.astype(jnp.bfloat16), grad_gate, grad_up)


def all_reduce_by_exchange(part, axes):
    device_count = lax.axis_size(axes)
    chunks = part.reshape(device_count, part.size // device_count)
    mine = jnp.sum(lax.all_to_all(chunks, axes, 0, 0, tiled=True), axis=0, keepdims=True)
    spread = jnp.broadcast_to(mine, chunks.shape)
    return lax.all_to_all(spread, axes, 0, 0, tiled=True).reshape(part.shape)


def reduce_scatter_by_exchange(parts, axis):
    replica_count = lax.axis_size(axis)
    rows = parts[0].shape[0] // replica_count
    blocks = jnp.stack([p.astype(jnp.bfloat16) for p in parts], axis=1)
    blocks = blocks.reshape((replica_count, rows) + blocks.shape[1:])
    blocks = blocks.reshape(replica_count, rows, len(parts), parts[0].shape[1])
    arrived = lax.all_to_all(blocks, axis, 0, 0, tiled=True)
    total = jnp.sum(arrived.astype(jnp.float32), axis=0)
    return tuple(total[:, i] for i in range(len(parts)))


def on_device(tokens, cotangent, expert_ids, router_w, w_gate, w_up, w_down):
    row_count, top_count = expert_ids.shape
    feature_count = tokens.shape[1]
    expert_count = lax.axis_size("expert")
    replica_count = lax.axis_size("dp")
    capacity = 2 * row_count * top_count // expert_count
    slot_count = expert_count * capacity
    expert_weights = (w_gate[0], w_up[0], w_down[0])
    logits = jnp.dot(tokens, router_w, preferred_element_type=jnp.float32)
    chosen = jnp.take_along_axis(logits, expert_ids, axis=1)
    route_probs = jax.nn.sigmoid(2.0 * chosen - jnp.sum(chosen, axis=1, keepdims=True))
    flat_slots = slot_positions(expert_ids, expert_count, capacity)
    owners = owner_table(flat_slots, slot_count)
    outbound = padded_rows(tokens, owners // top_count).reshape(
        expert_count, capacity, feature_count
    )
    received = lax.all_to_all(outbound, "expert", split_axis=0, concat_axis=0, tiled=True)
    expert_out, hidden, gate_pre, up_pre = expert_forward(received, expert_weights)
    received, expert_out, hidden, gate_pre, up_pre = (
        received,
        expert_out,
        hidden,
        gate_pre,
        up_pre,
    )
    returned = lax.all_to_all(
        expert_out, "expert", split_axis=0, concat_axis=0, tiled=True
    ).reshape(slot_count, feature_count)
    routed = returned[flat_slots].reshape(row_count, top_count, feature_count)
    output = jnp.sum(route_probs[:, :, None] * routed.astype(jnp.float32), axis=1).astype(
        jnp.bfloat16
    )
    grad_prob = jnp.einsum("td,tkd->tk", cotangent, routed, preferred_element_type=jnp.float32)
    mixed = jnp.sum(route_probs * grad_prob, axis=1, keepdims=True)
    grad_chosen = route_probs * (grad_prob - mixed)
    columns = jnp.arange(router_w.shape[1], dtype=jnp.int32)
    match = (expert_ids[:, :, None] == columns[None, None, :]).astype(jnp.float32)
    grad_logits = jnp.sum(grad_chosen[:, :, None] * match, axis=1).astype(jnp.bfloat16)
    router_part = jnp.dot(tokens.T, grad_logits, preferred_element_type=jnp.float32)
    router_grad = all_reduce_by_exchange(router_part, ("expert", "dp")) / replica_count
    weighted = (route_probs[:, :, None] * cotangent[:, None, :].astype(jnp.float32)).astype(
        jnp.bfloat16
    )
    weighted = weighted.reshape(row_count * top_count, feature_count)
    grad_out = padded_rows(weighted, owners).reshape(expert_count, capacity, feature_count)
    grad_recv = lax.all_to_all(grad_out, "expert", split_axis=0, concat_axis=0, tiled=True)
    grad_in, grad_gate, grad_up = expert_backward(grad_recv, gate_pre, up_pre, expert_weights)
    grad_back = lax.all_to_all(grad_in, "expert", split_axis=0, concat_axis=0, tiled=True).reshape(
        slot_count, feature_count
    )
    grad_tokens = jnp.sum(
        grad_back[flat_slots].reshape(row_count, top_count, feature_count).astype(jnp.float32),
        axis=1,
    )
    grad_tokens = grad_tokens + jnp.dot(grad_logits, router_w.T, preferred_element_type=jnp.float32)
    d_tokens = grad_tokens.astype(jnp.bfloat16)
    gate_part = jnp.einsum("nkd,nkh->dh", received, grad_gate, preferred_element_type=jnp.float32)
    up_part = jnp.einsum("nkd,nkh->dh", received, grad_up, preferred_element_type=jnp.float32)
    down_part = jnp.einsum("nkd,nkh->dh", grad_recv, hidden, preferred_element_type=jnp.float32)
    gate_total, up_total, down_total = reduce_scatter_by_exchange(
        (gate_part, up_part, down_part), "dp"
    )
    gate_grad = (gate_total / replica_count).astype(jnp.bfloat16)[None]
    up_grad = (up_total / replica_count).astype(jnp.bfloat16)[None]
    down_grad = (down_total / replica_count).astype(jnp.bfloat16)[None]
    return (output, d_tokens, router_grad, gate_grad, up_grad, down_grad)


def solution(mesh):
    placed = (
        P(("expert", "dp"), None),
        P(("expert", "dp"), None),
        P(("expert", "dp"), None),
        P(),
        P("expert", None, None),
        P("expert", None, None),
        P("expert", None, None),
    )
    return jax.shard_map(
        on_device,
        mesh=mesh,
        in_specs=placed,
        out_specs=(
            P(("expert", "dp"), None),
            P(("expert", "dp"), None),
            P(),
            P("expert", "dp", None),
            P("expert", "dp", None),
            P("expert", "dp", None),
        ),
        check_vma=False,
    )
```

```python
import jax
import jax.numpy as jnp
from jax import lax
from jax.sharding import PartitionSpec as P


def slot_positions(expert_ids, expert_count, capacity):
    row_count, top_count = expert_ids.shape
    flat_ids = expert_ids.reshape(row_count * top_count)
    onehot = (flat_ids[:, None] == jnp.arange(expert_count, dtype=jnp.int32)[None, :]).astype(
        jnp.int32
    )
    before = jnp.cumsum(onehot, axis=0) - onehot
    rank_in = jnp.sum(before * onehot, axis=1)
    return flat_ids * capacity + rank_in


def owner_table(flat_slots, slot_count):
    entry_count = flat_slots.shape[0]
    owners = jnp.full((slot_count,), entry_count, dtype=jnp.int32)
    return owners.at[flat_slots].set(jnp.arange(entry_count, dtype=jnp.int32))


def padded_rows(values, row_index):
    zero_row = jnp.zeros((1, values.shape[1]), values.dtype)
    return jnp.concatenate([values, zero_row], axis=0)[row_index]


def expert_forward(source_rows, expert_weights):
    gate_w, up_w, down_w = expert_weights
    gate_pre = jnp.einsum("...d,dh->...h", source_rows, gate_w, preferred_element_type=jnp.float32)
    up_pre = jnp.einsum("...d,dh->...h", source_rows, up_w, preferred_element_type=jnp.float32)
    hidden = (jax.nn.silu(gate_pre) * up_pre).astype(jnp.bfloat16)
    expert_out = jnp.einsum(
        "...h,dh->...d", hidden, down_w, preferred_element_type=jnp.float32
    ).astype(jnp.bfloat16)
    return (expert_out, hidden, gate_pre, up_pre)


def expert_backward(grad_rows, gate_pre, up_pre, expert_weights):
    gate_w, up_w, down_w = expert_weights
    grad_hidden = jnp.einsum("...d,dh->...h", grad_rows, down_w, preferred_element_type=jnp.float32)
    sigmoid_gate = jax.nn.sigmoid(gate_pre)
    grad_gate = (
        grad_hidden * up_pre * sigmoid_gate * (1.0 + gate_pre * (1.0 - sigmoid_gate))
    ).astype(jnp.bfloat16)
    grad_up = (grad_hidden * jax.nn.silu(gate_pre)).astype(jnp.bfloat16)
    grad_in = jnp.einsum("...h,dh->...d", grad_gate, gate_w, preferred_element_type=jnp.float32)
    grad_in = grad_in + jnp.einsum(
        "...h,dh->...d", grad_up, up_w, preferred_element_type=jnp.float32
    )
    return (grad_in.astype(jnp.bfloat16), grad_gate, grad_up)


def all_reduce_by_exchange(part, axes):
    device_count = lax.axis_size(axes)
    chunks = part.reshape(device_count, part.size // device_count)
    mine = jnp.sum(lax.all_to_all(chunks, axes, 0, 0, tiled=True), axis=0, keepdims=True)
    spread = jnp.broadcast_to(mine, chunks.shape)
    return lax.all_to_all(spread, axes, 0, 0, tiled=True).reshape(part.shape)


def reduce_scatter_by_exchange(parts, axis):
    replica_count = lax.axis_size(axis)
    rows = parts[0].shape[0] // replica_count
    blocks = jnp.stack([p.astype(jnp.bfloat16) for p in parts], axis=1)
    blocks = blocks.reshape((replica_count, rows) + blocks.shape[1:])
    me = lax.axis_index(axis)
    total = lax.dynamic_index_in_dim(blocks, me, axis=0, keepdims=False).astype(jnp.float32)
    for shift in range(1, replica_count):
        ahead = lax.dynamic_index_in_dim(blocks, (me + shift) % replica_count, axis=0, keepdims=False)
        pairs = [(j, (j + shift) % replica_count) for j in range(replica_count)]
        total = total + lax.ppermute(ahead, axis, pairs).astype(jnp.float32)
    return tuple(total[:, i] for i in range(len(parts)))


def on_device(tokens, cotangent, expert_ids, router_w, w_gate, w_up, w_down):
    row_count, top_count = expert_ids.shape
    feature_count = tokens.shape[1]
    expert_count = lax.axis_size("expert")
    replica_count = lax.axis_size("dp")
    capacity = 2 * row_count * top_count // expert_count
    slot_count = expert_count * capacity
    expert_weights = (w_gate[0], w_up[0], w_down[0])
    logits = jnp.dot(tokens, router_w, preferred_element_type=jnp.float32)
    chosen = jnp.take_along_axis(logits, expert_ids, axis=1)
    route_probs = jax.nn.sigmoid(2.0 * chosen - jnp.sum(chosen, axis=1, keepdims=True))
    flat_slots = slot_positions(expert_ids, expert_count, capacity)
    owners = owner_table(flat_slots, slot_count)
    outbound = padded_rows(tokens, owners // top_count).reshape(
        expert_count, capacity, feature_count
    )
    received = lax.all_to_all(outbound, "expert", split_axis=0, concat_axis=0, tiled=True)
    expert_out, hidden, gate_pre, up_pre = expert_forward(received, expert_weights)
    received, expert_out, hidden, gate_pre, up_pre = (
        received,
        expert_out,
        hidden,
        gate_pre,
        up_pre,
    )
    returned = lax.all_to_all(
        expert_out, "expert", split_axis=0, concat_axis=0, tiled=True
    ).reshape(slot_count, feature_count)
    routed = returned[flat_slots].reshape(row_count, top_count, feature_count)
    output = jnp.sum(route_probs[:, :, None] * routed.astype(jnp.float32), axis=1).astype(
        jnp.bfloat16
    )
    grad_prob = jnp.einsum("td,tkd->tk", cotangent, routed, preferred_element_type=jnp.float32)
    mixed = jnp.sum(route_probs * grad_prob, axis=1, keepdims=True)
    grad_chosen = route_probs * (grad_prob - mixed)
    columns = jnp.arange(router_w.shape[1], dtype=jnp.int32)
    match = (expert_ids[:, :, None] == columns[None, None, :]).astype(jnp.float32)
    grad_logits = jnp.sum(grad_chosen[:, :, None] * match, axis=1).astype(jnp.bfloat16)
    router_part = jnp.dot(tokens.T, grad_logits, preferred_element_type=jnp.float32)
    router_grad = all_reduce_by_exchange(router_part, ("expert", "dp")) / replica_count
    weighted = (route_probs[:, :, None] * cotangent[:, None, :].astype(jnp.float32)).astype(
        jnp.bfloat16
    )
    weighted = weighted.reshape(row_count * top_count, feature_count)
    grad_out = padded_rows(weighted, owners).reshape(expert_count, capacity, feature_count)
    grad_recv = lax.all_to_all(grad_out, "expert", split_axis=0, concat_axis=0, tiled=True)
    grad_in, grad_gate, grad_up = expert_backward(grad_recv, gate_pre, up_pre, expert_weights)
    grad_back = lax.all_to_all(grad_in, "expert", split_axis=0, concat_axis=0, tiled=True).reshape(
        slot_count, feature_count
    )
    grad_tokens = jnp.sum(
        grad_back[flat_slots].reshape(row_count, top_count, feature_count).astype(jnp.float32),
        axis=1,
    )
    grad_tokens = grad_tokens + jnp.dot(grad_logits, router_w.T, preferred_element_type=jnp.float32)
    d_tokens = grad_tokens.astype(jnp.bfloat16)
    gate_part = jnp.einsum("nkd,nkh->dh", received, grad_gate, preferred_element_type=jnp.float32)
    up_part = jnp.einsum("nkd,nkh->dh", received, grad_up, preferred_element_type=jnp.float32)
    down_part = jnp.einsum("nkd,nkh->dh", grad_recv, hidden, preferred_element_type=jnp.float32)
    (down_total,) = reduce_scatter_by_exchange((down_part,), "dp")
    gate_total, up_total = reduce_scatter_by_exchange((gate_part, up_part), "dp")
    gate_grad = (gate_total / replica_count).astype(jnp.bfloat16)[None]
    up_grad = (up_total / replica_count).astype(jnp.bfloat16)[None]
    down_grad = (down_total / replica_count).astype(jnp.bfloat16)[None]
    return (output, d_tokens, router_grad, gate_grad, up_grad, down_grad)


def solution(mesh):
    placed = (
        P(("expert", "dp"), None),
        P(("expert", "dp"), None),
        P(("expert", "dp"), None),
        P(),
        P("expert", None, None),
        P("expert", None, None),
        P("expert", None, None),
    )
    return jax.shard_map(
        on_device,
        mesh=mesh,
        in_specs=placed,
        out_specs=(
            P(("expert", "dp"), None),
            P(("expert", "dp"), None),
            P(),
            P("expert", "dp", None),
            P("expert", "dp", None),
            P("expert", "dp", None),
        ),
        check_vma=False,
    )
```

```python
import jax
import jax.numpy as jnp
from jax import lax
from jax.sharding import PartitionSpec as P


def slot_positions(expert_ids, expert_count, capacity):
    row_count, top_count = expert_ids.shape
    flat_ids = expert_ids.reshape(row_count * top_count)
    onehot = (flat_ids[:, None] == jnp.arange(expert_count, dtype=jnp.int32)[None, :]).astype(
        jnp.int32
    )
    before = jnp.cumsum(onehot, axis=0) - onehot
    rank_in = jnp.sum(before * onehot, axis=1)
    return flat_ids * capacity + rank_in


def owner_table(flat_slots, slot_count):
    entry_count = flat_slots.shape[0]
    owners = jnp.full((slot_count,), entry_count, dtype=jnp.int32)
    return owners.at[flat_slots].set(jnp.arange(entry_count, dtype=jnp.int32))


def padded_rows(values, row_index):
    zero_row = jnp.zeros((1, values.shape[1]), values.dtype)
    return jnp.concatenate([values, zero_row], axis=0)[row_index]


def expert_forward(source_rows, expert_weights):
    gate_w, up_w, down_w = expert_weights
    gate_pre = jnp.einsum("...d,dh->...h", source_rows, gate_w, preferred_element_type=jnp.float32)
    up_pre = jnp.einsum("...d,dh->...h", source_rows, up_w, preferred_element_type=jnp.float32)
    hidden = (jax.nn.silu(gate_pre) * up_pre).astype(jnp.bfloat16)
    expert_out = jnp.einsum(
        "...h,dh->...d", hidden, down_w, preferred_element_type=jnp.float32
    ).astype(jnp.bfloat16)
    return (expert_out, hidden, gate_pre, up_pre)


def expert_backward(grad_rows, gate_pre, up_pre, expert_weights):
    gate_w, up_w, down_w = expert_weights
    grad_hidden = jnp.einsum("...d,dh->...h", grad_rows, down_w, preferred_element_type=jnp.float32)
    sigmoid_gate = jax.nn.sigmoid(gate_pre)
    grad_gate = (
        grad_hidden * up_pre * sigmoid_gate * (1.0 + gate_pre * (1.0 - sigmoid_gate))
    ).astype(jnp.bfloat16)
    grad_up = (grad_hidden * jax.nn.silu(gate_pre)).astype(jnp.bfloat16)
    grad_in = jnp.einsum("...h,dh->...d", grad_gate, gate_w, preferred_element_type=jnp.float32)
    grad_in = grad_in + jnp.einsum(
        "...h,dh->...d", grad_up, up_w, preferred_element_type=jnp.float32
    )
    return (grad_in.astype(jnp.bfloat16), grad_gate, grad_up)


def all_reduce_by_exchange(part, axes):
    device_count = lax.axis_size(axes)
    chunks = part.reshape(device_count, part.size // device_count)
    mine = jnp.sum(lax.all_to_all(chunks, axes, 0, 0, tiled=True), axis=0, keepdims=True)
    spread = jnp.broadcast_to(mine, chunks.shape)
    return lax.all_to_all(spread, axes, 0, 0, tiled=True).reshape(part.shape)


def reduce_scatter_by_exchange(parts, axis):
    replica_count = lax.axis_size(axis)
    rows = parts[0].shape[0] // replica_count
    blocks = jnp.stack([p.astype(jnp.bfloat16) for p in parts], axis=1)
    blocks = blocks.reshape((replica_count, rows) + blocks.shape[1:])
    blocks = blocks.reshape(replica_count, rows, len(parts), parts[0].shape[1])
    arrived = lax.all_to_all(blocks, axis, 0, 0, tiled=True)
    total = jnp.sum(arrived.astype(jnp.float32), axis=0)
    return tuple(total[:, i] for i in range(len(parts)))


def on_device(tokens, cotangent, expert_ids, router_w, w_gate, w_up, w_down):
    row_count, top_count = expert_ids.shape
    feature_count = tokens.shape[1]
    expert_count = lax.axis_size("expert")
    replica_count = lax.axis_size("dp")
    capacity = 2 * row_count * top_count // expert_count
    slot_count = expert_count * capacity
    expert_weights = (w_gate[0], w_up[0], w_down[0])
    logits = jnp.dot(tokens, router_w, preferred_element_type=jnp.float32)
    chosen = jnp.take_along_axis(logits, expert_ids, axis=1)
    route_probs = jax.nn.sigmoid(2.0 * chosen - jnp.sum(chosen, axis=1, keepdims=True))
    flat_slots = slot_positions(expert_ids, expert_count, capacity)
    owners = owner_table(flat_slots, slot_count)
    outbound = padded_rows(tokens, owners // top_count).reshape(
        expert_count, capacity, feature_count
    )
    received = lax.all_to_all(outbound, "expert", split_axis=0, concat_axis=0, tiled=True)
    expert_out, hidden, gate_pre, up_pre = expert_forward(received, expert_weights)
    received, expert_out, hidden, gate_pre, up_pre = (
        received,
        expert_out,
        hidden,
        gate_pre,
        up_pre,
    )
    returned = lax.all_to_all(
        expert_out, "expert", split_axis=0, concat_axis=0, tiled=True
    ).reshape(slot_count, feature_count)
    routed = returned[flat_slots].reshape(row_count, top_count, feature_count)
    output = jnp.sum(route_probs[:, :, None] * routed.astype(jnp.float32), axis=1).astype(
        jnp.bfloat16
    )
    grad_prob = jnp.einsum("td,tkd->tk", cotangent, routed, preferred_element_type=jnp.float32)
    mixed = jnp.sum(route_probs * grad_prob, axis=1, keepdims=True)
    grad_chosen = route_probs * (grad_prob - mixed)
    columns = jnp.arange(router_w.shape[1], dtype=jnp.int32)
    match = (expert_ids[:, :, None] == columns[None, None, :]).astype(jnp.float32)
    grad_logits = jnp.sum(grad_chosen[:, :, None] * match, axis=1).astype(jnp.bfloat16)
    router_part = jnp.dot(tokens.T, grad_logits, preferred_element_type=jnp.float32)
    router_grad = all_reduce_by_exchange(router_part, ("expert", "dp")) / replica_count
    weighted = (route_probs[:, :, None] * cotangent[:, None, :].astype(jnp.float32)).astype(
        jnp.bfloat16
    )
    weighted = weighted.reshape(row_count * top_count, feature_count)
    grad_out = padded_rows(weighted, owners).reshape(expert_count, capacity, feature_count)
    grad_recv = lax.all_to_all(grad_out, "expert", split_axis=0, concat_axis=0, tiled=True)
    grad_in, grad_gate, grad_up = expert_backward(grad_recv, gate_pre, up_pre, expert_weights)
    grad_back = lax.all_to_all(grad_in, "expert", split_axis=0, concat_axis=0, tiled=True).reshape(
        slot_count, feature_count
    )
    grad_tokens = jnp.sum(
        grad_back[flat_slots].reshape(row_count, top_count, feature_count).astype(jnp.float32),
        axis=1,
    )
    grad_tokens = grad_tokens + jnp.dot(grad_logits, router_w.T, preferred_element_type=jnp.float32)
    d_tokens = grad_tokens.astype(jnp.bfloat16)
    gate_part = jnp.einsum("nkd,nkh->dh", received, grad_gate, preferred_element_type=jnp.float32)
    up_part = jnp.einsum("nkd,nkh->dh", received, grad_up, preferred_element_type=jnp.float32)
    down_part = jnp.einsum("nkd,nkh->dh", grad_recv, hidden, preferred_element_type=jnp.float32)
    down_total = lax.psum_scatter(
        down_part.astype(jnp.bfloat16), "dp", scatter_dimension=0, tiled=True
    ).astype(jnp.float32)
    gate_total, up_total = reduce_scatter_by_exchange((gate_part, up_part), "dp")
    gate_grad = (gate_total / replica_count).astype(jnp.bfloat16)[None]
    up_grad = (up_total / replica_count).astype(jnp.bfloat16)[None]
    down_grad = (down_total / replica_count).astype(jnp.bfloat16)[None]
    return (output, d_tokens, router_grad, gate_grad, up_grad, down_grad)


def solution(mesh):
    placed = (
        P(("expert", "dp"), None),
        P(("expert", "dp"), None),
        P(("expert", "dp"), None),
        P(),
        P("expert", None, None),
        P("expert", None, None),
        P("expert", None, None),
    )
    return jax.shard_map(
        on_device,
        mesh=mesh,
        in_specs=placed,
        out_specs=(
            P(("expert", "dp"), None),
            P(("expert", "dp"), None),
            P(),
            P("expert", "dp", None),
            P("expert", "dp", None),
            P("expert", "dp", None),
        ),
        check_vma=False,
    )
```

```python
import jax
import jax.numpy as jnp
from jax import lax
from jax.sharding import PartitionSpec as P


def slot_positions(expert_ids, expert_count, capacity):
    row_count, top_count = expert_ids.shape
    flat_ids = expert_ids.reshape(row_count * top_count)
    onehot = (flat_ids[:, None] == jnp.arange(expert_count, dtype=jnp.int32)[None, :]).astype(
        jnp.int32
    )
    before = jnp.cumsum(onehot, axis=0) - onehot
    rank_in = jnp.sum(before * onehot, axis=1)
    return flat_ids * capacity + rank_in


def owner_table(flat_slots, slot_count):
    entry_count = flat_slots.shape[0]
    owners = jnp.full((slot_count,), entry_count, dtype=jnp.int32)
    return owners.at[flat_slots].set(jnp.arange(entry_count, dtype=jnp.int32))


def padded_rows(values, row_index):
    zero_row = jnp.zeros((1, values.shape[1]), values.dtype)
    return jnp.concatenate([values, zero_row], axis=0)[row_index]


def expert_forward(source_rows, expert_weights):
    gate_w, up_w, down_w = expert_weights
    gate_pre = jnp.einsum("...d,dh->...h", source_rows, gate_w, preferred_element_type=jnp.float32)
    up_pre = jnp.einsum("...d,dh->...h", source_rows, up_w, preferred_element_type=jnp.float32)
    hidden = (jax.nn.silu(gate_pre) * up_pre).astype(jnp.bfloat16)
    expert_out = jnp.einsum(
        "...h,dh->...d", hidden, down_w, preferred_element_type=jnp.float32
    ).astype(jnp.bfloat16)
    return (expert_out, hidden, gate_pre, up_pre)


def expert_backward(grad_rows, gate_pre, up_pre, expert_weights):
    gate_w, up_w, down_w = expert_weights
    grad_hidden = jnp.einsum("...d,dh->...h", grad_rows, down_w, preferred_element_type=jnp.float32)
    sigmoid_gate = jax.nn.sigmoid(gate_pre)
    grad_gate = (
        grad_hidden * up_pre * sigmoid_gate * (1.0 + gate_pre * (1.0 - sigmoid_gate))
    ).astype(jnp.bfloat16)
    grad_up = (grad_hidden * jax.nn.silu(gate_pre)).astype(jnp.bfloat16)
    grad_in = jnp.einsum("...h,dh->...d", grad_gate, gate_w, preferred_element_type=jnp.float32)
    grad_in = grad_in + jnp.einsum(
        "...h,dh->...d", grad_up, up_w, preferred_element_type=jnp.float32
    )
    return (grad_in.astype(jnp.bfloat16), grad_gate, grad_up)


def all_reduce_by_exchange(part, axes):
    device_count = lax.axis_size(axes)
    chunks = part.reshape(device_count, part.size // device_count)
    mine = jnp.sum(lax.all_to_all(chunks, axes, 0, 0, tiled=True), axis=0, keepdims=True)
    spread = jnp.broadcast_to(mine, chunks.shape)
    return lax.all_to_all(spread, axes, 0, 0, tiled=True).reshape(part.shape)


def reduce_scatter_by_exchange(parts, axis):
    replica_count = lax.axis_size(axis)
    rows = parts[0].shape[0] // replica_count
    blocks = jnp.stack([p.astype(jnp.bfloat16) for p in parts], axis=1)
    blocks = blocks.reshape((replica_count, rows) + blocks.shape[1:])
    blocks = blocks.reshape(replica_count, rows, len(parts), parts[0].shape[1])
    arrived = lax.all_to_all(blocks, axis, 0, 0, tiled=True)
    total = jnp.sum(arrived.astype(jnp.float32), axis=0)
    return tuple(total[:, i] for i in range(len(parts)))


def on_device(tokens, cotangent, expert_ids, router_w, w_gate, w_up, w_down):
    row_count, top_count = expert_ids.shape
    feature_count = tokens.shape[1]
    expert_count = lax.axis_size("expert")
    replica_count = lax.axis_size("dp")
    capacity = 2 * row_count * top_count // expert_count
    slot_count = expert_count * capacity
    expert_weights = (w_gate[0], w_up[0], w_down[0])
    logits = jnp.dot(tokens, router_w, preferred_element_type=jnp.float32)
    chosen = jnp.take_along_axis(logits, expert_ids, axis=1)
    route_probs = jax.nn.sigmoid(2.0 * chosen - jnp.sum(chosen, axis=1, keepdims=True))
    flat_slots = slot_positions(expert_ids, expert_count, capacity)
    owners = owner_table(flat_slots, slot_count)
    outbound = padded_rows(tokens, owners // top_count).reshape(
        expert_count, capacity, feature_count
    )
    received = lax.all_to_all(outbound, "expert", split_axis=0, concat_axis=0, tiled=True)
    weighted = (route_probs[:, :, None] * cotangent[:, None, :].astype(jnp.float32)).astype(
        jnp.bfloat16
    )
    weighted = weighted.reshape(row_count * top_count, feature_count)
    grad_out = padded_rows(weighted, owners).reshape(expert_count, capacity, feature_count)
    grad_recv = lax.all_to_all(grad_out, "expert", split_axis=0, concat_axis=0, tiled=True)
    expert_out, hidden, gate_pre, up_pre = expert_forward(received, expert_weights)
    expert_out, grad_recv = lax.optimization_barrier((expert_out, grad_recv))
    returned = lax.all_to_all(
        expert_out, "expert", split_axis=0, concat_axis=0, tiled=True
    ).reshape(slot_count, feature_count)
    routed = returned[flat_slots].reshape(row_count, top_count, feature_count)
    output = jnp.sum(route_probs[:, :, None] * routed.astype(jnp.float32), axis=1).astype(
        jnp.bfloat16
    )
    grad_prob = jnp.einsum("td,tkd->tk", cotangent, routed, preferred_element_type=jnp.float32)
    mixed = jnp.sum(route_probs * grad_prob, axis=1, keepdims=True)
    grad_chosen = route_probs * (grad_prob - mixed)
    columns = jnp.arange(router_w.shape[1], dtype=jnp.int32)
    match = (expert_ids[:, :, None] == columns[None, None, :]).astype(jnp.float32)
    grad_logits = jnp.sum(grad_chosen[:, :, None] * match, axis=1).astype(jnp.bfloat16)
    router_part = jnp.dot(tokens.T, grad_logits, preferred_element_type=jnp.float32)
    router_grad = all_reduce_by_exchange(router_part, ("expert", "dp")) / replica_count
    grad_in, grad_gate, grad_up = expert_backward(grad_recv, gate_pre, up_pre, expert_weights)
    grad_back = lax.all_to_all(grad_in, "expert", split_axis=0, concat_axis=0, tiled=True).reshape(
        slot_count, feature_count
    )
    grad_tokens = jnp.sum(
        grad_back[flat_slots].reshape(row_count, top_count, feature_count).astype(jnp.float32),
        axis=1,
    )
    grad_tokens = grad_tokens + jnp.dot(grad_logits, router_w.T, preferred_element_type=jnp.float32)
    d_tokens = grad_tokens.astype(jnp.bfloat16)
    gate_part = jnp.einsum("nkd,nkh->dh", received, grad_gate, preferred_element_type=jnp.float32)
    up_part = jnp.einsum("nkd,nkh->dh", received, grad_up, preferred_element_type=jnp.float32)
    down_part = jnp.einsum("nkd,nkh->dh", grad_recv, hidden, preferred_element_type=jnp.float32)
    down_total = lax.psum_scatter(
        down_part.astype(jnp.bfloat16), "dp", scatter_dimension=0, tiled=True
    ).astype(jnp.float32)
    gate_total, up_total = reduce_scatter_by_exchange((gate_part, up_part), "dp")
    gate_grad = (gate_total / replica_count).astype(jnp.bfloat16)[None]
    up_grad = (up_total / replica_count).astype(jnp.bfloat16)[None]
    down_grad = (down_total / replica_count).astype(jnp.bfloat16)[None]
    return (output, d_tokens, router_grad, gate_grad, up_grad, down_grad)


def solution(mesh):
    placed = (
        P(("expert", "dp"), None),
        P(("expert", "dp"), None),
        P(("expert", "dp"), None),
        P(),
        P("expert", None, None),
        P("expert", None, None),
        P("expert", None, None),
    )
    return jax.shard_map(
        on_device,
        mesh=mesh,
        in_specs=placed,
        out_specs=(
            P(("expert", "dp"), None),
            P(("expert", "dp"), None),
            P(),
            P("expert", "dp", None),
            P("expert", "dp", None),
            P("expert", "dp", None),
        ),
        check_vma=False,
    )
```

```python
import jax
import jax.numpy as jnp
from jax import lax
from jax.sharding import PartitionSpec as P


def slot_positions(expert_ids, expert_count, capacity):
    row_count, top_count = expert_ids.shape
    flat_ids = expert_ids.reshape(row_count * top_count)
    onehot = (flat_ids[:, None] == jnp.arange(expert_count, dtype=jnp.int32)[None, :]).astype(
        jnp.int32
    )
    before = jnp.cumsum(onehot, axis=0) - onehot
    rank_in = jnp.sum(before * onehot, axis=1)
    return flat_ids * capacity + rank_in


def owner_table(flat_slots, slot_count):
    entry_count = flat_slots.shape[0]
    owners = jnp.full((slot_count,), entry_count, dtype=jnp.int32)
    return owners.at[flat_slots].set(jnp.arange(entry_count, dtype=jnp.int32))


def padded_rows(values, row_index):
    zero_row = jnp.zeros((1, values.shape[1]), values.dtype)
    return jnp.concatenate([values, zero_row], axis=0)[row_index]


def expert_forward(source_rows, expert_weights):
    gate_w, up_w, down_w = expert_weights
    gate_pre = jnp.einsum("...d,dh->...h", source_rows, gate_w, preferred_element_type=jnp.float32)
    up_pre = jnp.einsum("...d,dh->...h", source_rows, up_w, preferred_element_type=jnp.float32)
    hidden = (jax.nn.silu(gate_pre) * up_pre).astype(jnp.bfloat16)
    expert_out = jnp.einsum(
        "...h,dh->...d", hidden, down_w, preferred_element_type=jnp.float32
    ).astype(jnp.bfloat16)
    return (expert_out, hidden, gate_pre, up_pre)


def expert_backward(grad_rows, gate_pre, up_pre, expert_weights):
    gate_w, up_w, down_w = expert_weights
    grad_hidden = jnp.einsum("...d,dh->...h", grad_rows, down_w, preferred_element_type=jnp.float32)
    sigmoid_gate = jax.nn.sigmoid(gate_pre)
    grad_gate = (
        grad_hidden * up_pre * sigmoid_gate * (1.0 + gate_pre * (1.0 - sigmoid_gate))
    ).astype(jnp.bfloat16)
    grad_up = (grad_hidden * jax.nn.silu(gate_pre)).astype(jnp.bfloat16)
    grad_in = jnp.einsum("...h,dh->...d", grad_gate, gate_w, preferred_element_type=jnp.float32)
    grad_in = grad_in + jnp.einsum(
        "...h,dh->...d", grad_up, up_w, preferred_element_type=jnp.float32
    )
    return (grad_in.astype(jnp.bfloat16), grad_gate, grad_up)


def all_reduce_by_exchange(part, axes):
    device_count = lax.axis_size(axes)
    chunks = part.reshape(device_count, part.size // device_count)
    mine = jnp.sum(lax.all_to_all(chunks, axes, 0, 0, tiled=True), axis=0, keepdims=True)
    spread = jnp.broadcast_to(mine, chunks.shape)
    return lax.all_to_all(spread, axes, 0, 0, tiled=True).reshape(part.shape)


def reduce_scatter_by_ring(parts, axis):
    replica_count = lax.axis_size(axis)
    rows = parts[0].shape[0] // replica_count
    blocks = jnp.stack([p.astype(jnp.bfloat16) for p in parts], axis=1)
    blocks = blocks.reshape((replica_count, rows) + blocks.shape[1:])
    half = blocks.shape[-1] // 2
    rows_along = replica_count // 2
    ring = [2 * z for z in range(rows_along)] + [2 * z + 1 for z in reversed(range(rows_along))]
    place = [ring.index(i) for i in range(replica_count)]
    ring_at = jnp.asarray(ring, jnp.int32)
    pos = jnp.asarray(place, jnp.int32)[lax.axis_index(axis)]
    forward = [(ring[q], ring[(q + 1) % replica_count]) for q in range(replica_count)]
    backward = [(ring[q], ring[(q - 1) % replica_count]) for q in range(replica_count)]

    def block(step, lower):
        owner = ring_at[(pos + step) % replica_count]
        rows_of = lax.dynamic_index_in_dim(blocks, owner, axis=0, keepdims=False)
        return (rows_of[..., :half] if lower else rows_of[..., half:]).astype(jnp.float32)

    ahead = block(-1, True)
    behind = block(1, False)
    for step in range(1, replica_count):
        ahead = lax.ppermute(ahead.astype(jnp.bfloat16), axis, forward).astype(jnp.float32)
        ahead = ahead + block(-1 - step, True)
        behind = lax.ppermute(behind.astype(jnp.bfloat16), axis, backward).astype(jnp.float32)
        behind = behind + block(1 + step, False)
    total = jnp.concatenate([ahead, behind], axis=-1)
    return tuple(total[:, i] for i in range(len(parts)))


def on_device(tokens, cotangent, expert_ids, router_w, w_gate, w_up, w_down):
    row_count, top_count = expert_ids.shape
    feature_count = tokens.shape[1]
    expert_count = lax.axis_size("expert")
    replica_count = lax.axis_size("dp")
    capacity = 2 * row_count * top_count // expert_count
    slot_count = expert_count * capacity
    expert_weights = (w_gate[0], w_up[0], w_down[0])
    logits = jnp.dot(tokens, router_w, preferred_element_type=jnp.float32)
    chosen = jnp.take_along_axis(logits, expert_ids, axis=1)
    route_probs = jax.nn.sigmoid(2.0 * chosen - jnp.sum(chosen, axis=1, keepdims=True))
    flat_slots = slot_positions(expert_ids, expert_count, capacity)
    owners = owner_table(flat_slots, slot_count)
    outbound = padded_rows(tokens, owners // top_count).reshape(
        expert_count, capacity, feature_count
    )
    received = lax.all_to_all(outbound, "expert", split_axis=0, concat_axis=0, tiled=True)
    weighted = (route_probs[:, :, None] * cotangent[:, None, :].astype(jnp.float32)).astype(
        jnp.bfloat16
    )
    weighted = weighted.reshape(row_count * top_count, feature_count)
    grad_out = padded_rows(weighted, owners).reshape(expert_count, capacity, feature_count)
    grad_recv = lax.all_to_all(grad_out, "expert", split_axis=0, concat_axis=0, tiled=True)
    expert_out, hidden, gate_pre, up_pre = expert_forward(received, expert_weights)
    expert_out, grad_recv = lax.optimization_barrier((expert_out, grad_recv))
    returned = lax.all_to_all(
        expert_out, "expert", split_axis=0, concat_axis=0, tiled=True
    ).reshape(slot_count, feature_count)
    routed = returned[flat_slots].reshape(row_count, top_count, feature_count)
    output = jnp.sum(route_probs[:, :, None] * routed.astype(jnp.float32), axis=1).astype(
        jnp.bfloat16
    )
    grad_prob = jnp.einsum("td,tkd->tk", cotangent, routed, preferred_element_type=jnp.float32)
    mixed = jnp.sum(route_probs * grad_prob, axis=1, keepdims=True)
    grad_chosen = route_probs * (grad_prob - mixed)
    columns = jnp.arange(router_w.shape[1], dtype=jnp.int32)
    match = (expert_ids[:, :, None] == columns[None, None, :]).astype(jnp.float32)
    grad_logits = jnp.sum(grad_chosen[:, :, None] * match, axis=1).astype(jnp.bfloat16)
    router_part = jnp.dot(tokens.T, grad_logits, preferred_element_type=jnp.float32)
    router_grad = all_reduce_by_exchange(router_part, ("expert", "dp")) / replica_count
    grad_in, grad_gate, grad_up = expert_backward(grad_recv, gate_pre, up_pre, expert_weights)
    grad_back = lax.all_to_all(grad_in, "expert", split_axis=0, concat_axis=0, tiled=True).reshape(
        slot_count, feature_count
    )
    grad_tokens = jnp.sum(
        grad_back[flat_slots].reshape(row_count, top_count, feature_count).astype(jnp.float32),
        axis=1,
    )
    grad_tokens = grad_tokens + jnp.dot(grad_logits, router_w.T, preferred_element_type=jnp.float32)
    d_tokens = grad_tokens.astype(jnp.bfloat16)
    gate_part = jnp.einsum("nkd,nkh->dh", received, grad_gate, preferred_element_type=jnp.float32)
    up_part = jnp.einsum("nkd,nkh->dh", received, grad_up, preferred_element_type=jnp.float32)
    down_part = jnp.einsum("nkd,nkh->dh", grad_recv, hidden, preferred_element_type=jnp.float32)
    down_total = lax.psum_scatter(
        down_part.astype(jnp.bfloat16), "dp", scatter_dimension=0, tiled=True
    ).astype(jnp.float32)
    gate_total, up_total = reduce_scatter_by_ring((gate_part, up_part), "dp")
    gate_grad = (gate_total / replica_count).astype(jnp.bfloat16)[None]
    up_grad = (up_total / replica_count).astype(jnp.bfloat16)[None]
    down_grad = (down_total / replica_count).astype(jnp.bfloat16)[None]
    return (output, d_tokens, router_grad, gate_grad, up_grad, down_grad)


def solution(mesh):
    placed = (
        P(("expert", "dp"), None),
        P(("expert", "dp"), None),
        P(("expert", "dp"), None),
        P(),
        P("expert", None, None),
        P("expert", None, None),
        P("expert", None, None),
    )
    return jax.shard_map(
        on_device,
        mesh=mesh,
        in_specs=placed,
        out_specs=(
            P(("expert", "dp"), None),
            P(("expert", "dp"), None),
            P(),
            P("expert", "dp", None),
            P("expert", "dp", None),
            P("expert", "dp", None),
        ),
        check_vma=False,
    )
```

```python
import jax
import jax.numpy as jnp
from jax import lax
from jax.sharding import PartitionSpec as P


def slot_positions(expert_ids, expert_count, capacity):
    row_count, top_count = expert_ids.shape
    flat_ids = expert_ids.reshape(row_count * top_count)
    onehot = (flat_ids[:, None] == jnp.arange(expert_count, dtype=jnp.int32)[None, :]).astype(
        jnp.int32
    )
    before = jnp.cumsum(onehot, axis=0) - onehot
    rank_in = jnp.sum(before * onehot, axis=1)
    return flat_ids * capacity + rank_in


def owner_table(flat_slots, slot_count):
    entry_count = flat_slots.shape[0]
    owners = jnp.full((slot_count,), entry_count, dtype=jnp.int32)
    return owners.at[flat_slots].set(jnp.arange(entry_count, dtype=jnp.int32))


def padded_rows(values, row_index):
    zero_row = jnp.zeros((1, values.shape[1]), values.dtype)
    return jnp.concatenate([values, zero_row], axis=0)[row_index]


def expert_forward(source_rows, expert_weights):
    gate_w, up_w, down_w = expert_weights
    gate_pre = jnp.einsum("...d,dh->...h", source_rows, gate_w, preferred_element_type=jnp.float32)
    up_pre = jnp.einsum("...d,dh->...h", source_rows, up_w, preferred_element_type=jnp.float32)
    hidden = (jax.nn.silu(gate_pre) * up_pre).astype(jnp.bfloat16)
    expert_out = jnp.einsum(
        "...h,dh->...d", hidden, down_w, preferred_element_type=jnp.float32
    ).astype(jnp.bfloat16)
    return (expert_out, hidden, gate_pre, up_pre)


def expert_backward(grad_rows, gate_pre, up_pre, expert_weights):
    gate_w, up_w, down_w = expert_weights
    grad_hidden = jnp.einsum("...d,dh->...h", grad_rows, down_w, preferred_element_type=jnp.float32)
    sigmoid_gate = jax.nn.sigmoid(gate_pre)
    grad_gate = (
        grad_hidden * up_pre * sigmoid_gate * (1.0 + gate_pre * (1.0 - sigmoid_gate))
    ).astype(jnp.bfloat16)
    grad_up = (grad_hidden * jax.nn.silu(gate_pre)).astype(jnp.bfloat16)
    grad_in = jnp.einsum("...h,dh->...d", grad_gate, gate_w, preferred_element_type=jnp.float32)
    grad_in = grad_in + jnp.einsum(
        "...h,dh->...d", grad_up, up_w, preferred_element_type=jnp.float32
    )
    return (grad_in.astype(jnp.bfloat16), grad_gate, grad_up)


def all_reduce_by_exchange(part, axes):
    device_count = lax.axis_size(axes)
    chunks = part.reshape(device_count, part.size // device_count)
    mine = jnp.sum(lax.all_to_all(chunks, axes, 0, 0, tiled=True), axis=0, keepdims=True)
    spread = jnp.broadcast_to(mine, chunks.shape)
    return lax.all_to_all(spread, axes, 0, 0, tiled=True).reshape(part.shape)


def reduce_scatter_by_exchange(parts, axis):
    replica_count = lax.axis_size(axis)
    rows = parts[0].shape[0] // replica_count
    blocks = jnp.stack([p.astype(jnp.bfloat16) for p in parts], axis=1)
    blocks = blocks.reshape((replica_count, rows) + blocks.shape[1:])
    blocks = blocks.reshape(replica_count, rows, len(parts), parts[0].shape[1])
    arrived = lax.all_to_all(blocks, axis, 0, 0, tiled=True)
    total = jnp.sum(arrived.astype(jnp.float32), axis=0)
    return tuple(total[:, i] for i in range(len(parts)))


def on_device(tokens, cotangent, expert_ids, router_w, w_gate, w_up, w_down):
    row_count, top_count = expert_ids.shape
    feature_count = tokens.shape[1]
    expert_count = lax.axis_size("expert")
    replica_count = lax.axis_size("dp")
    capacity = 2 * row_count * top_count // expert_count
    slot_count = expert_count * capacity
    expert_weights = (w_gate[0], w_up[0], w_down[0])
    logits = jnp.dot(tokens, router_w, preferred_element_type=jnp.float32)
    chosen = jnp.take_along_axis(logits, expert_ids, axis=1)
    route_probs = jax.nn.sigmoid(2.0 * chosen - jnp.sum(chosen, axis=1, keepdims=True))
    flat_slots = slot_positions(expert_ids, expert_count, capacity)
    owners = owner_table(flat_slots, slot_count)
    outbound = padded_rows(tokens, owners // top_count).reshape(
        expert_count, capacity, feature_count
    )
    received = lax.all_to_all(outbound, "expert", split_axis=0, concat_axis=0, tiled=True)
    weighted = (route_probs[:, :, None] * cotangent[:, None, :].astype(jnp.float32)).astype(
        jnp.bfloat16
    )
    weighted = weighted.reshape(row_count * top_count, feature_count)
    grad_out = padded_rows(weighted, owners).reshape(expert_count, capacity, feature_count)
    grad_recv = lax.all_to_all(grad_out, "expert", split_axis=0, concat_axis=0, tiled=True)
    expert_out, hidden, gate_pre, up_pre = expert_forward(received, expert_weights)
    expert_out, grad_recv = lax.optimization_barrier((expert_out, grad_recv))
    returned = lax.all_to_all(
        expert_out, "expert", split_axis=0, concat_axis=0, tiled=True
    ).reshape(slot_count, feature_count)
    routed = returned[flat_slots].reshape(row_count, top_count, feature_count)
    output = jnp.sum(route_probs[:, :, None] * routed.astype(jnp.float32), axis=1).astype(
        jnp.bfloat16
    )
    grad_prob = jnp.einsum("td,tkd->tk", cotangent, routed, preferred_element_type=jnp.float32)
    mixed = jnp.sum(route_probs * grad_prob, axis=1, keepdims=True)
    grad_chosen = route_probs * (grad_prob - mixed)
    columns = jnp.arange(router_w.shape[1], dtype=jnp.int32)
    match = (expert_ids[:, :, None] == columns[None, None, :]).astype(jnp.float32)
    grad_logits = jnp.sum(grad_chosen[:, :, None] * match, axis=1).astype(jnp.bfloat16)
    router_part = jnp.dot(tokens.T, grad_logits, preferred_element_type=jnp.float32)
    router_grad = all_reduce_by_exchange(router_part, ("expert", "dp")) / replica_count
    grad_in, grad_gate, grad_up = expert_backward(grad_recv, gate_pre, up_pre, expert_weights)
    grad_back = lax.all_to_all(grad_in, "expert", split_axis=0, concat_axis=0, tiled=True).reshape(
        slot_count, feature_count
    )
    grad_tokens = jnp.sum(
        grad_back[flat_slots].reshape(row_count, top_count, feature_count).astype(jnp.float32),
        axis=1,
    )
    grad_tokens = grad_tokens + jnp.dot(grad_logits, router_w.T, preferred_element_type=jnp.float32)
    d_tokens = grad_tokens.astype(jnp.bfloat16)
    gate_part = jnp.einsum("nkd,nkh->dh", received, grad_gate, preferred_element_type=jnp.float32)
    up_part = jnp.einsum("nkd,nkh->dh", received, grad_up, preferred_element_type=jnp.float32)
    down_part = jnp.einsum("nkd,nkh->dh", grad_recv, hidden, preferred_element_type=jnp.float32)
    hidden_count = up_part.shape[1]
    split = hidden_count // 3
    on_sparse = jnp.concatenate([down_part, up_part[:, :split]], axis=1)
    on_sparse = lax.psum_scatter(
        on_sparse.astype(jnp.bfloat16), "dp", scatter_dimension=0, tiled=True
    ).astype(jnp.float32)
    (exchanged,) = reduce_scatter_by_exchange(
        (jnp.concatenate([gate_part, up_part[:, split:]], axis=1),), "dp"
    )
    down_total = on_sparse[:, :hidden_count]
    gate_total = exchanged[:, :hidden_count]
    up_total = jnp.concatenate([on_sparse[:, hidden_count:], exchanged[:, hidden_count:]], axis=1)
    gate_grad = (gate_total / replica_count).astype(jnp.bfloat16)[None]
    up_grad = (up_total / replica_count).astype(jnp.bfloat16)[None]
    down_grad = (down_total / replica_count).astype(jnp.bfloat16)[None]
    return (output, d_tokens, router_grad, gate_grad, up_grad, down_grad)


def solution(mesh):
    placed = (
        P(("expert", "dp"), None),
        P(("expert", "dp"), None),
        P(("expert", "dp"), None),
        P(),
        P("expert", None, None),
        P("expert", None, None),
        P("expert", None, None),
    )
    return jax.shard_map(
        on_device,
        mesh=mesh,
        in_specs=placed,
        out_specs=(
            P(("expert", "dp"), None),
            P(("expert", "dp"), None),
            P(),
            P("expert", "dp", None),
            P("expert", "dp", None),
            P("expert", "dp", None),
        ),
        check_vma=False,
    )
```

```python
import jax
import jax.numpy as jnp
from jax import lax
from jax.sharding import PartitionSpec as P


def slot_positions(expert_ids, expert_count, capacity):
    row_count, top_count = expert_ids.shape
    flat_ids = expert_ids.reshape(row_count * top_count)
    onehot = (flat_ids[:, None] == jnp.arange(expert_count, dtype=jnp.int32)[None, :]).astype(
        jnp.int32
    )
    before = jnp.cumsum(onehot, axis=0) - onehot
    rank_in = jnp.sum(before * onehot, axis=1)
    return flat_ids * capacity + rank_in


def owner_table(flat_slots, slot_count):
    entry_count = flat_slots.shape[0]
    owners = jnp.full((slot_count,), entry_count, dtype=jnp.int32)
    return owners.at[flat_slots].set(jnp.arange(entry_count, dtype=jnp.int32))


def padded_rows(values, row_index):
    zero_row = jnp.zeros((1, values.shape[1]), values.dtype)
    return jnp.concatenate([values, zero_row], axis=0)[row_index]


def expert_forward(source_rows, expert_weights):
    gate_w, up_w, down_w = expert_weights
    gate_pre = jnp.einsum("...d,dh->...h", source_rows, gate_w, preferred_element_type=jnp.float32)
    up_pre = jnp.einsum("...d,dh->...h", source_rows, up_w, preferred_element_type=jnp.float32)
    hidden = (jax.nn.silu(gate_pre) * up_pre).astype(jnp.bfloat16)
    expert_out = jnp.einsum(
        "...h,dh->...d", hidden, down_w, preferred_element_type=jnp.float32
    ).astype(jnp.bfloat16)
    return (expert_out, hidden, gate_pre, up_pre)


def expert_backward(grad_rows, gate_pre, up_pre, expert_weights):
    gate_w, up_w, down_w = expert_weights
    grad_hidden = jnp.einsum("...d,dh->...h", grad_rows, down_w, preferred_element_type=jnp.float32)
    sigmoid_gate = jax.nn.sigmoid(gate_pre)
    grad_gate = (
        grad_hidden * up_pre * sigmoid_gate * (1.0 + gate_pre * (1.0 - sigmoid_gate))
    ).astype(jnp.bfloat16)
    grad_up = (grad_hidden * jax.nn.silu(gate_pre)).astype(jnp.bfloat16)
    grad_in = jnp.einsum("...h,dh->...d", grad_gate, gate_w, preferred_element_type=jnp.float32)
    grad_in = grad_in + jnp.einsum(
        "...h,dh->...d", grad_up, up_w, preferred_element_type=jnp.float32
    )
    return (grad_in.astype(jnp.bfloat16), grad_gate, grad_up)


def all_reduce_by_exchange(part, axes):
    device_count = lax.axis_size(axes)
    chunks = part.reshape(device_count, part.size // device_count)
    mine = jnp.sum(lax.all_to_all(chunks, axes, 0, 0, tiled=True), axis=0, keepdims=True)
    spread = jnp.broadcast_to(mine, chunks.shape)
    return lax.all_to_all(spread, axes, 0, 0, tiled=True).reshape(part.shape)


def reduce_scatter_by_exchange(parts, axis):
    replica_count = lax.axis_size(axis)
    pieces, row_count, width = parts.shape
    blocks = parts.astype(jnp.bfloat16).reshape(
        pieces, replica_count, row_count // replica_count, width
    )
    arrived = lax.all_to_all(blocks, axis, 1, 1, tiled=True)
    return jnp.sum(arrived.astype(jnp.float32), axis=1)


def on_device(tokens, cotangent, expert_ids, router_w, w_gate, w_up, w_down):
    row_count, top_count = expert_ids.shape
    feature_count = tokens.shape[1]
    expert_count = lax.axis_size("expert")
    replica_count = lax.axis_size("dp")
    capacity = 2 * row_count * top_count // expert_count
    slot_count = expert_count * capacity
    expert_weights = (w_gate[0], w_up[0], w_down[0])
    logits = jnp.dot(tokens, router_w, preferred_element_type=jnp.float32)
    chosen = jnp.take_along_axis(logits, expert_ids, axis=1)
    route_probs = jax.nn.sigmoid(2.0 * chosen - jnp.sum(chosen, axis=1, keepdims=True))
    flat_slots = slot_positions(expert_ids, expert_count, capacity)
    owners = owner_table(flat_slots, slot_count)
    outbound = padded_rows(tokens, owners // top_count).reshape(
        expert_count, capacity, feature_count
    )
    received = lax.all_to_all(outbound, "expert", split_axis=0, concat_axis=0, tiled=True)
    weighted = (route_probs[:, :, None] * cotangent[:, None, :].astype(jnp.float32)).astype(
        jnp.bfloat16
    )
    weighted = weighted.reshape(row_count * top_count, feature_count)
    grad_out = padded_rows(weighted, owners).reshape(expert_count, capacity, feature_count)
    grad_recv = lax.all_to_all(grad_out, "expert", split_axis=0, concat_axis=0, tiled=True)
    expert_out, hidden, gate_pre, up_pre = expert_forward(received, expert_weights)
    expert_out, grad_recv = lax.optimization_barrier((expert_out, grad_recv))
    returned = lax.all_to_all(
        expert_out, "expert", split_axis=0, concat_axis=0, tiled=True
    ).reshape(slot_count, feature_count)
    routed = returned[flat_slots].reshape(row_count, top_count, feature_count)
    output = jnp.sum(route_probs[:, :, None] * routed.astype(jnp.float32), axis=1).astype(
        jnp.bfloat16
    )
    grad_prob = jnp.einsum("td,tkd->tk", cotangent, routed, preferred_element_type=jnp.float32)
    mixed = jnp.sum(route_probs * grad_prob, axis=1, keepdims=True)
    grad_chosen = route_probs * (grad_prob - mixed)
    columns = jnp.arange(router_w.shape[1], dtype=jnp.int32)
    match = (expert_ids[:, :, None] == columns[None, None, :]).astype(jnp.float32)
    grad_logits = jnp.sum(grad_chosen[:, :, None] * match, axis=1).astype(jnp.bfloat16)
    router_part = jnp.dot(tokens.T, grad_logits, preferred_element_type=jnp.float32)
    router_grad = all_reduce_by_exchange(router_part, ("expert", "dp")) / replica_count
    grad_in, grad_gate, grad_up = expert_backward(grad_recv, gate_pre, up_pre, expert_weights)
    grad_back = lax.all_to_all(grad_in, "expert", split_axis=0, concat_axis=0, tiled=True).reshape(
        slot_count, feature_count
    )
    grad_tokens = jnp.sum(
        grad_back[flat_slots].reshape(row_count, top_count, feature_count).astype(jnp.float32),
        axis=1,
    )
    grad_tokens = grad_tokens + jnp.dot(grad_logits, router_w.T, preferred_element_type=jnp.float32)
    d_tokens = grad_tokens.astype(jnp.bfloat16)
    grad_pair = jnp.stack([grad_gate, grad_up], axis=0)
    pair_part = jnp.einsum(
        "nkd,pnkh->pdh", received, grad_pair, preferred_element_type=jnp.float32
    )
    down_part = jnp.einsum("nkd,nkh->dh", grad_recv, hidden, preferred_element_type=jnp.float32)
    down_total = lax.psum_scatter(
        down_part.astype(jnp.bfloat16), "dp", scatter_dimension=0, tiled=True
    ).astype(jnp.float32)
    pair_total = reduce_scatter_by_exchange(pair_part, "dp")
    gate_total, up_total = pair_total[0], pair_total[1]
    gate_grad = (gate_total / replica_count).astype(jnp.bfloat16)[None]
    up_grad = (up_total / replica_count).astype(jnp.bfloat16)[None]
    down_grad = (down_total / replica_count).astype(jnp.bfloat16)[None]
    return (output, d_tokens, router_grad, gate_grad, up_grad, down_grad)


def solution(mesh):
    placed = (
        P(("expert", "dp"), None),
        P(("expert", "dp"), None),
        P(("expert", "dp"), None),
        P(),
        P("expert", None, None),
        P("expert", None, None),
        P("expert", None, None),
    )
    return jax.shard_map(
        on_device,
        mesh=mesh,
        in_specs=placed,
        out_specs=(
            P(("expert", "dp"), None),
            P(("expert", "dp"), None),
            P(),
            P("expert", "dp", None),
            P("expert", "dp", None),
            P("expert", "dp", None),
        ),
        check_vma=False,
    )
```

```python
import jax
import jax.numpy as jnp
from jax import lax
from jax.sharding import PartitionSpec as P


def slot_positions(expert_ids, expert_count, capacity):
    row_count, top_count = expert_ids.shape
    flat_ids = expert_ids.reshape(row_count * top_count)
    onehot = (flat_ids[:, None] == jnp.arange(expert_count, dtype=jnp.int32)[None, :]).astype(
        jnp.int32
    )
    before = jnp.cumsum(onehot, axis=0) - onehot
    rank_in = jnp.sum(before * onehot, axis=1)
    return flat_ids * capacity + rank_in


def owner_table(flat_slots, slot_count):
    entry_count = flat_slots.shape[0]
    owners = jnp.full((slot_count,), entry_count, dtype=jnp.int32)
    return owners.at[flat_slots].set(jnp.arange(entry_count, dtype=jnp.int32))


def padded_rows(values, row_index):
    zero_row = jnp.zeros((1, values.shape[1]), values.dtype)
    return jnp.concatenate([values, zero_row], axis=0)[row_index]


def expert_forward(source_rows, expert_weights):
    gate_w, up_w, down_w = expert_weights
    gate_pre = jnp.einsum("...d,dh->...h", source_rows, gate_w, preferred_element_type=jnp.float32)
    up_pre = jnp.einsum("...d,dh->...h", source_rows, up_w, preferred_element_type=jnp.float32)
    hidden = (jax.nn.silu(gate_pre) * up_pre).astype(jnp.bfloat16)
    expert_out = jnp.einsum(
        "...h,dh->...d", hidden, down_w, preferred_element_type=jnp.float32
    ).astype(jnp.bfloat16)
    return (expert_out, hidden, gate_pre, up_pre)


def expert_backward(grad_rows, gate_pre, up_pre, expert_weights):
    gate_w, up_w, down_w = expert_weights
    grad_hidden = jnp.einsum("...d,dh->...h", grad_rows, down_w, preferred_element_type=jnp.float32)
    sigmoid_gate = jax.nn.sigmoid(gate_pre)
    grad_gate = (
        grad_hidden * up_pre * sigmoid_gate * (1.0 + gate_pre * (1.0 - sigmoid_gate))
    ).astype(jnp.bfloat16)
    grad_up = (grad_hidden * jax.nn.silu(gate_pre)).astype(jnp.bfloat16)
    grad_in = jnp.einsum("...h,dh->...d", grad_gate, gate_w, preferred_element_type=jnp.float32)
    grad_in = grad_in + jnp.einsum(
        "...h,dh->...d", grad_up, up_w, preferred_element_type=jnp.float32
    )
    return (grad_in.astype(jnp.bfloat16), grad_gate, grad_up)


def all_reduce_by_exchange(part, axes):
    device_count = lax.axis_size(axes)
    chunks = part.reshape(device_count, part.size // device_count)
    mine = jnp.sum(lax.all_to_all(chunks, axes, 0, 0, tiled=True), axis=0, keepdims=True)
    spread = jnp.broadcast_to(mine, chunks.shape)
    return lax.all_to_all(spread, axes, 0, 0, tiled=True).reshape(part.shape)


def reduce_scatter_by_exchange(parts, axis):
    replica_count = lax.axis_size(axis)
    rows = parts[0].shape[0] // replica_count
    blocks = jnp.stack([p.astype(jnp.bfloat16) for p in parts], axis=1)
    blocks = blocks.reshape((replica_count, rows) + blocks.shape[1:])
    blocks = blocks.reshape(replica_count, rows, len(parts), parts[0].shape[1])
    arrived = lax.all_to_all(blocks, axis, 0, 0, tiled=True)
    total = (jnp.sum(arrived.astype(jnp.float32), axis=0) / replica_count).astype(jnp.bfloat16)
    return tuple(total[:, i] for i in range(len(parts)))


def on_device(tokens, cotangent, expert_ids, router_w, w_gate, w_up, w_down):
    row_count, top_count = expert_ids.shape
    feature_count = tokens.shape[1]
    expert_count = lax.axis_size("expert")
    replica_count = lax.axis_size("dp")
    capacity = 2 * row_count * top_count // expert_count
    slot_count = expert_count * capacity
    expert_weights = (w_gate[0], w_up[0], w_down[0])
    logits = jnp.dot(tokens, router_w, preferred_element_type=jnp.float32)
    chosen = jnp.take_along_axis(logits, expert_ids, axis=1)
    route_probs = jax.nn.sigmoid(2.0 * chosen - jnp.sum(chosen, axis=1, keepdims=True))
    flat_slots = slot_positions(expert_ids, expert_count, capacity)
    owners = owner_table(flat_slots, slot_count)
    outbound = padded_rows(tokens, owners // top_count).reshape(
        expert_count, capacity, feature_count
    )
    received = lax.all_to_all(outbound, "expert", split_axis=0, concat_axis=0, tiled=True)
    weighted = (route_probs[:, :, None] * cotangent[:, None, :].astype(jnp.float32)).astype(
        jnp.bfloat16
    )
    weighted = weighted.reshape(row_count * top_count, feature_count)
    grad_out = padded_rows(weighted, owners).reshape(expert_count, capacity, feature_count)
    grad_recv = lax.all_to_all(grad_out, "expert", split_axis=0, concat_axis=0, tiled=True)
    expert_out, hidden, gate_pre, up_pre = expert_forward(received, expert_weights)
    expert_out, grad_recv = lax.optimization_barrier((expert_out, grad_recv))
    returned = lax.all_to_all(
        expert_out, "expert", split_axis=0, concat_axis=0, tiled=True
    ).reshape(slot_count, feature_count)
    routed = returned[flat_slots].reshape(row_count, top_count, feature_count)
    output = jnp.sum(route_probs[:, :, None] * routed.astype(jnp.float32), axis=1).astype(
        jnp.bfloat16
    )
    grad_prob = jnp.einsum("td,tkd->tk", cotangent, routed, preferred_element_type=jnp.float32)
    mixed = jnp.sum(route_probs * grad_prob, axis=1, keepdims=True)
    grad_chosen = route_probs * (grad_prob - mixed)
    columns = jnp.arange(router_w.shape[1], dtype=jnp.int32)
    match = (expert_ids[:, :, None] == columns[None, None, :]).astype(jnp.float32)
    grad_logits = jnp.sum(grad_chosen[:, :, None] * match, axis=1).astype(jnp.bfloat16)
    router_part = jnp.dot(tokens.T, grad_logits, preferred_element_type=jnp.float32)
    router_grad = all_reduce_by_exchange(router_part, ("expert", "dp")) / replica_count
    grad_in, grad_gate, grad_up = expert_backward(grad_recv, gate_pre, up_pre, expert_weights)
    grad_back = lax.all_to_all(grad_in, "expert", split_axis=0, concat_axis=0, tiled=True).reshape(
        slot_count, feature_count
    )
    grad_tokens = jnp.sum(
        grad_back[flat_slots].reshape(row_count, top_count, feature_count).astype(jnp.float32),
        axis=1,
    )
    grad_tokens = grad_tokens + jnp.dot(grad_logits, router_w.T, preferred_element_type=jnp.float32)
    d_tokens = grad_tokens.astype(jnp.bfloat16)
    gate_part = jnp.einsum("nkd,nkh->dh", received, grad_gate, preferred_element_type=jnp.float32)
    up_part = jnp.einsum("nkd,nkh->dh", received, grad_up, preferred_element_type=jnp.float32)
    down_part = jnp.einsum("nkd,nkh->dh", grad_recv, hidden, preferred_element_type=jnp.float32)
    down_total = lax.psum_scatter(
        down_part.astype(jnp.bfloat16), "dp", scatter_dimension=0, tiled=True
    ).astype(jnp.float32)
    gate_total, up_total = reduce_scatter_by_exchange((gate_part, up_part), "dp")
    gate_grad = gate_total[None]
    up_grad = up_total[None]
    down_grad = (down_total / replica_count).astype(jnp.bfloat16)[None]
    return (output, d_tokens, router_grad, gate_grad, up_grad, down_grad)


def solution(mesh):
    placed = (
        P(("expert", "dp"), None),
        P(("expert", "dp"), None),
        P(("expert", "dp"), None),
        P(),
        P("expert", None, None),
        P("expert", None, None),
        P("expert", None, None),
    )
    return jax.shard_map(
        on_device,
        mesh=mesh,
        in_specs=placed,
        out_specs=(
            P(("expert", "dp"), None),
            P(("expert", "dp"), None),
            P(),
            P("expert", "dp", None),
            P("expert", "dp", None),
            P("expert", "dp", None),
        ),
        check_vma=False,
    )
```
